32 devices in a mesh: replica: 8 (over z, x), tensor: 4 (over y, core).
Axes of the slice: x: 2, y: 2, z: 4, core: 2. Of those that a mesh axis runs over, the one named last changes fastest.
Arguments:
- hidden: bfloat16 [256, 8192], P('replica'), may hold values from -16 to 16
- q_weight: bfloat16 [8192, 4096], P(None, 'tensor'), may hold values from -0.0625 to 0.0625
- q_gain: float32 [128], replicated, may hold values from 0.1 to 1.9
- o_weight: bfloat16 [4096, 8192], P('tensor'), may hold values from -0.125 to 0.125
- attn_gate: float32 [1], replicated, may hold values from 0.5 to 1.5
- key_codes: bfloat16 [64, 128, 1024], P('replica', 'tensor'), may hold values from -96 to 96
- value_codes: bfloat16 [64, 128, 1024], P('replica', 'tensor'), may hold values from -96 to 96
- key_scales: bfloat16 [64, 4, 8], P('replica', 'tensor'), may hold values from 0.02 to 8
- value_scales: bfloat16 [64, 4, 8], P('replica', 'tensor'), may hold values from 0.019897461 to 0.119628906
- lengths: int32 [64], P('replica'), may hold values from 32 to 128
- dest_replica: int32 [8, 6], replicated, may hold values from 0 to 7, as said below
- move_slot: int32 [8, 6], P('replica'), may hold values from 0 to 7, as said below
Outputs:
- mixed: bfloat16 [256, 8192], P('replica', 'tensor')
- new_keys: bfloat16 [64, 128, 1024], P('replica', 'tensor')
- new_values: bfloat16 [64, 128, 1024], P('replica', 'tensor')
- new_key_scales: bfloat16 [64, 4, 8], P('replica', 'tensor')
- new_value_scales: bfloat16 [64, 4, 8], P('replica', 'tensor')
The draws below stay inside these ranges and needn't reach their ends.
Inputs may be any that keep to these rules, and one draw needn't show every extreme that they name: For each j the column dest_replica[:, j] names every replica once, so each replica receives exactly 6 requests, at most one from each replica; a request may stay on its own replica. `move_slot`: the 6 slots of one replica are different.
All inputs are finite; a program needn't handle non-finite values.
Results may differ from the reference program's by a relative error of at most 0.0065.
Values may be sent and summed in bfloat16 or wider, within the bound.
A program may use at most 64 MiB of HBM per device.

```python
import math
import jax
import jax.numpy as jnp
from jax import lax

D = 8192
HQ = 32
KVH = 8
HD = 128
IMG_DEV = 32
REQ_REP = 8
SPEC = 4
MOVE = 6
REPLICAS = 8
REQUESTS = 64
IMG = 128
TSHARDS = 4
ROWS = 256


def draw_hidden(key, part):
    first, second = jax.random.split(jax.random.fold_in(key, 11), 2)
    scales = jnp.exp(jax.random.uniform(first, (ROWS, 1), jnp.float32, math.log(0.25), math.log(4.0)))
    values = jnp.clip(jax.random.normal(second, (ROWS, D), jnp.float32), -4.0, 4.0) * scales
    return values.astype(jnp.bfloat16)


def draw_key_scales(key, part):
    first = jax.random.fold_in(jax.random.fold_in(key, 23), 0)
    base = jnp.exp(jax.random.uniform(first, (REQUESTS, TSHARDS, KVH), jnp.float32, math.log(0.02), math.log(0.12)))
    return base.astype(jnp.bfloat16)


def draw_dest_replica(key, part):
    first, second, third = jax.random.split(jax.random.fold_in(key, 37), 3)
    relabel = jax.random.permutation(first, REPLICAS)
    order = jax.random.permutation(second, REPLICAS)
    offsets = jax.random.permutation(third, REPLICAS)[:MOVE]
    return relabel[(order[:, None] + offsets[None, :]) % REPLICAS].astype(jnp.int32)


def draw_move_slot(key, part):
    keys = jax.random.split(jax.random.fold_in(key, 41), REPLICAS)
    return jax.vmap(lambda item: jax.random.permutation(item, REQ_REP)[:MOVE])(keys).astype(jnp.int32)


def place_ends(entries, own_key, low, largest):
    index_at = [jax.random.randint(jax.random.fold_in(own_key, axis), (), 0, length) for axis, length in enumerate(entries.shape)]
    longest = entries.shape.index(max(entries.shape))
    beside = index_at[:longest] + [(index_at[longest] + 1) % entries.shape[longest]] + index_at[longest + 1:]
    return entries.at[tuple(index_at)].set(low).at[tuple(beside)].set(largest)


def strengthened(array, rng, source, target, parts, factor):
    def block_of(axis_at):
        return (jnp.arange(array.shape[axis_at]) // (array.shape[axis_at] // parts)).reshape((-1,) + (1,) * (array.ndim - 1 - axis_at))

    near = jax.random.permutation(rng, parts)[block_of(target)]
    far = (block_of(target) + parts // 2) % parts
    return jnp.where((block_of(source) == near) | (block_of(source) == far), factor * array, array)


def block_scale(own_key, shape, shards, least, largest):
    def one(axis_at, blocks):
        steps = jax.random.uniform(jax.random.fold_in(jax.random.fold_in(own_key, 6), axis_at), (blocks,), jnp.float32, least / len(shards), largest / len(shards))
        return jnp.repeat(jnp.exp(steps), shape[axis_at] // blocks).reshape((-1,) + (1,) * (len(shape) - axis_at - 1))

    gain = one(*shards[0])
    for cut in shards[1:]:
        gain = gain * one(*cut)
    return gain


def centred(key, dims, spread, limit, cuts=(), kind=jnp.bfloat16):
    loudness = block_scale(key, dims, cuts, -0.22, 0.18) if cuts else 1.0
    array = jax.random.normal(key, dims, jnp.float32) * spread * loudness
    return jnp.minimum(jnp.maximum(array, -limit), limit).astype(kind)


def gaussian_with(rng, shape, scale, most, shards, heavy, kind=jnp.bfloat16):
    array = scale * jax.random.normal(rng, shape, jnp.float32)
    if shards:
        array = array * block_scale(rng, shape, shards, -0.22, 0.18)
    return jnp.clip(strengthened(array, jax.random.fold_in(rng, 3), *heavy), -most, most).astype(kind)


def setup_inputs(seed: int = 0) -> dict:
    seeds = jax.random.split(jax.random.key(seed), 13)
    hidden = draw_hidden(jax.random.fold_in(seeds[12], 71), 0)
    q_weight = centred(seeds[1], (D, HQ * HD), D ** -0.5, 0.0625, ((1, 4),))
    q_gain = jnp.clip(1.0 + 0.18 * jax.random.normal(seeds[2], (HD,), jnp.float32), 0.1, 1.9)
    o_weight = gaussian_with(seeds[3], (HQ * HD, D), (HQ * HD) ** -0.5, 0.125, ((0, 4),), (0, 1, 4, 2.0))
    attn_gate = jnp.clip(jax.random.uniform(seeds[4], (1,), jnp.float32, 0.5, 1.5), 0.5, 1.5)
    key_codes = centred(seeds[5], (REQUESTS, IMG, KVH * HD), 16.0, 96.0, ((0, 8), (1, 4)))
    value_codes = centred(seeds[6], (REQUESTS, IMG, KVH * HD), 16.0, 96.0, ((0, 8), (1, 4)))
    key_scales = draw_key_scales(jax.random.fold_in(seeds[12], 71), 0)
    value_scales = jnp.clip(jnp.exp(math.log(0.119628906) - 1.7938024 * jax.random.uniform(seeds[8], (REQUESTS, TSHARDS, KVH), jnp.float32) ** block_scale(seeds[8], (REQUESTS, TSHARDS, KVH), ((0, 8), (1, 4)), -0.2, 0.2)), 0.019897461, 0.119628906).astype(jnp.bfloat16)
    lengths = place_ends(jax.random.randint(seeds[9], (REQUESTS,), IMG // 4, IMG + 1), jax.random.fold_in(seeds[9], 1), IMG // 4, IMG).astype(jnp.int32)
    dest_replica = draw_dest_replica(jax.random.fold_in(seeds[12], 71), 0)
    move_slot = draw_move_slot(jax.random.fold_in(seeds[12], 71), 0)
    return dict(hidden=hidden, q_weight=q_weight, q_gain=q_gain, o_weight=o_weight, attn_gate=attn_gate, key_codes=key_codes, value_codes=value_codes, key_scales=key_scales, value_scales=value_scales, lengths=lengths, dest_replica=dest_replica, move_slot=move_slot)


NEGATIVE = -1e+30
EPSILON = 1e-06

def one_request(item):
    query, keys, values, key_scale, value_scale, length = item
    keys = keys.reshape(TSHARDS, IMG_DEV, KVH, HD).astype(jnp.float32)
    values = values.reshape(TSHARDS, IMG_DEV, KVH, HD).astype(jnp.float32)
    scores = jnp.einsum('sngd,btnd->sngbt', query.astype(jnp.float32), keys, precision=lax.Precision.HIGHEST)
    scores = scores * key_scale.astype(jnp.float32).T[None, :, None, :, None]
    position = jnp.arange(IMG, dtype=jnp.int32).reshape(TSHARDS, IMG_DEV)
    valid = position < length
    block_max = lax.optimization_barrier(jnp.max(jnp.where(valid, scores, NEGATIVE), axis=-1))
    weights = jnp.where(valid, jnp.exp(scores - block_max[..., None]), 0.0)
    block_sum = lax.optimization_barrier(jnp.sum(weights, axis=-1))
    rounded = weights.astype(jnp.bfloat16).astype(jnp.float32)
    block_out = jnp.einsum('sngbt,btnd->sngbd', rounded, values, precision=lax.Precision.HIGHEST)
    block_out = block_out * value_scale.astype(jnp.float32).T[None, :, None, :, None]
    top = lax.optimization_barrier(jnp.max(block_max, axis=-1))
    factor = jnp.exp(block_max - top[..., None])
    total = lax.optimization_barrier(jnp.sum(block_sum * factor, axis=-1))
    summed = lax.optimization_barrier(jnp.sum(block_out * factor[..., None], axis=3))
    return (summed / total[..., None]).astype(jnp.bfloat16)

def reference(hidden, q_weight, q_gain, o_weight, attn_gate, key_codes, value_codes, key_scales, value_scales, lengths, dest_replica, move_slot):
    projected = jnp.dot(hidden, q_weight, preferred_element_type=jnp.float32).reshape(ROWS, HQ, HD)
    projected = projected * lax.rsqrt(lax.optimization_barrier(jnp.mean(projected * projected, axis=-1, keepdims=True)) + EPSILON)
    query = (projected * q_gain.astype(jnp.float32) * HD ** (-0.5)).astype(jnp.bfloat16)
    grouped = query.reshape(REQUESTS, SPEC, KVH, HQ // KVH, HD)
    attended = lax.map(one_request, (grouped, key_codes, value_codes, key_scales, value_scales, lengths))
    attended = attended.reshape(ROWS, HQ * HD)
    summed = jnp.dot(attended, o_weight, preferred_element_type=jnp.float32)
    mixed = (hidden.astype(jnp.float32) + jnp.tanh(attn_gate[0]) * summed).astype(jnp.bfloat16)
    columns = jnp.arange(MOVE, dtype=jnp.int32)[None, :]
    source_rows = (jnp.arange(REPLICAS, dtype=jnp.int32)[:, None] * REQ_REP + move_slot).reshape(-1)
    target_rows = (dest_replica * REQ_REP + move_slot[dest_replica, columns]).reshape(-1)
    order = jnp.arange(REQUESTS, dtype=jnp.int32).at[target_rows].set(source_rows)
    return (mixed, key_codes[order], value_codes[order], key_scales[order], value_scales[order])
```

```python
import functools

import jax
import jax.numpy as jnp
from jax import lax
from jax.experimental import pallas as pl
from jax.experimental.pallas import tpu as pltpu
from jax.sharding import PartitionSpec as P

NEGATIVE = -1e30
EPSILON = 1e-06
LANES = 128
MESH = pl.DeviceIdType.MESH


def kernel(
    replicas,
    shards,
    heads_here,
    group,
    chunks,
    dest_ref,
    slot_ref,
    len_ref,
    gate_ref,
    gain_ref,
    scale_ref,
    hidden_hbm,
    qw_hbm,
    ow_hbm,
    keys_hbm,
    values_hbm,
    mixed_ref,
    new_keys_hbm,
    new_values_hbm,
    new_scale_ref,
    hidden,
    qw,
    ow,
    keys,
    values,
    send_codes,
    recv_keys,
    recv_values,
    send_scale,
    recv_scale,
    placed,
    acc,
    queries,
    part_own,
    part_out,
    part_in,
    stat_own,
    stat_out,
    stat_in,
    attended,
    share_own,
    share_out,
    share_in,
    scale_rows,
    bias,
    load_sem,
    qw_sem,
    ow_sem,
    code_send_sem,
    code_recv_sem,
    scale_send_sem,
    scale_recv_sem,
    query_send_sem,
    query_recv_sem,
    part_send_sem,
    part_recv_sem,
    stat_send_sem,
    stat_recv_sem,
    share_send_sem,
    share_recv_sem,
    out_sem,
):
    here = lax.axis_index("replica")
    rank = lax.axis_index("tensor")
    held, span, _ = keys.shape
    moves = slot_ref.shape[1]
    rows, width = hidden.shape
    drafts = rows // held
    per = min(heads_here, group)
    kv_here = heads_here // per
    tall = per * rows
    deep = qw_hbm.shape[0] // chunks
    high = ow_hbm.shape[0] // chunks
    share = width // shards

    loads = [
        pltpu.make_async_copy(keys_hbm, keys, load_sem.at[0]),
        pltpu.make_async_copy(values_hbm, values, load_sem.at[1]),
        pltpu.make_async_copy(hidden_hbm, hidden, load_sem.at[2]),
    ]
    for load in loads:
        load.start()

    def load_qw(c):
        at = pl.ds(pl.multiple_of(c * deep, deep), deep)
        return pltpu.make_async_copy(qw_hbm.at[at], qw.at[at], qw_sem.at[c])

    def load_ow(c):
        at = pl.ds(pl.multiple_of(c * high, high), high)
        return pltpu.make_async_copy(ow_hbm.at[at], ow.at[at], ow_sem.at[c])

    for c in range(chunks):
        load_qw(c).start()

    far = [lax.rem(here + k, replicas) for k in range(1, replicas)]
    partner = rank + 1 - 2 * lax.rem(rank, 2)
    near = []
    for j in range(1, shards // 2):
        pair = lax.rem(rank // 2 + j, shards // 2) * 2
        near += [pair + lax.rem(rank + c, 2) for c in range(2)]
    arrive_order = [partner] + near
    leave_order = near + [partner]

    barrier = pltpu.get_barrier_semaphore()
    for other in far:
        pl.semaphore_signal(barrier, inc=1, device_id=(other, rank), device_id_type=MESH)
    for other in leave_order:
        pl.semaphore_signal(barrier, inc=1, device_id=(here, other), device_id_type=MESH)

    slots = [slot_ref[0, j] for j in range(moves)]

    def leaving(target):
        found = jnp.int32(0)
        for j in range(moves):
            found = jnp.where(dest_ref[here, j] == target, slots[j], found)
        return found

    loads[0].wait()
    loads[1].wait()
    for other in far:
        slot = leaving(other)
        send_codes[0, other] = keys[slot]
        send_codes[1, other] = values[slot]
        send_scale[other] = jnp.broadcast_to(scale_ref[slot], send_scale.shape[1:])
    recv_codes = (recv_keys, recv_values)
    recv_keys[here] = keys[0]
    recv_values[here] = values[0]
    recv_scale[here] = jnp.broadcast_to(scale_ref[0], send_scale.shape[1:])

    pl.semaphore_wait(barrier, replicas - 1 + shards - 1)

    def move_codes(which, k):
        other = far[k]
        return pltpu.make_async_remote_copy(
            src_ref=send_codes.at[which, other],
            dst_ref=recv_codes[which].at[here],
            send_sem=code_send_sem.at[which, other],
            recv_sem=code_recv_sem.at[which, here],
            device_id=(other, rank),
            device_id_type=MESH,
        )

    def take_codes(which, k):
        other = far[k]
        return pltpu.make_async_remote_copy(
            src_ref=send_codes.at[which, other],
            dst_ref=recv_codes[which].at[other],
            send_sem=code_send_sem.at[which, other],
            recv_sem=code_recv_sem.at[which, other],
            device_id=(other, rank),
            device_id_type=MESH,
        )

    def move_scale(k, at):
        other = far[k]
        return pltpu.make_async_remote_copy(
            src_ref=send_scale.at[other],
            dst_ref=recv_scale.at[at],
            send_sem=scale_send_sem.at[other],
            recv_sem=scale_recv_sem.at[at],
            device_id=(other, rank),
            device_id_type=MESH,
        )

    for which in range(2):
        for k in range(replicas - 1):
            move_codes(which, k).start()
    for k in range(replicas - 1):
        move_scale(k, here).start()

    lane = lax.broadcasted_iota(jnp.int32, (tall, LANES), 1)
    row_request = lax.rem(lax.broadcasted_iota(jnp.int32, (tall, LANES), 0), rows) // drafts
    table = jnp.zeros((tall, LANES), jnp.float32)
    for r in range(held):
        table = jnp.where(row_request == r, scale_ref[r], table)
    scale_rows[...] = table
    wide = held * span
    column = lax.broadcasted_iota(jnp.int32, (tall, wide), 1)
    column_request = column // span
    row_of = lax.rem(lax.broadcasted_iota(jnp.int32, (tall, wide), 0), rows) // drafts
    limit = jnp.zeros((tall, wide), jnp.int32)
    for r in range(held):
        limit = jnp.where(column_request == r, len_ref[r], limit)
    position = rank * span + lax.rem(column, span)
    bias[...] = jnp.where((position < limit) & (row_of == column_request), 0.0, NEGATIVE)

    loads[2].wait()
    acc[...] = jnp.zeros_like(acc)

    @pl.loop(0, chunks)
    def _(c):
        load_qw(c).wait()
        load_ow(c).start()
        at = pl.ds(pl.multiple_of(c * deep, deep), deep)
        acc[...] += jnp.dot(hidden[:, at], qw[at, :], preferred_element_type=jnp.float32)

    for h in range(heads_here):
        at = slice(h * LANES, (h + 1) * LANES)
        head = acc[:, at]
        head = head * lax.rsqrt(jnp.mean(head * head, axis=-1, keepdims=True) + EPSILON)
        queries[rank, :, at] = (head * gain_ref[...] * LANES ** (-0.5)).astype(jnp.bfloat16)

    def swap(source, target, send_sem, recv_sem, other, from_at, to_at):
        return pltpu.make_async_remote_copy(
            src_ref=source.at[from_at],
            dst_ref=target.at[to_at],
            send_sem=send_sem.at[other],
            recv_sem=recv_sem.at[to_at],
            device_id=(here, other),
            device_id_type=MESH,
        )

    def query_copy(other, from_at, to_at):
        return swap(queries, queries, query_send_sem, query_recv_sem, other, from_at, to_at)

    def part_copy(other, to_at):
        return swap(part_out, part_in, part_send_sem, part_recv_sem, other, other, to_at)

    def stat_copy(other, to_at):
        return swap(stat_out, stat_in, stat_send_sem, stat_recv_sem, other, other, to_at)

    def share_copy(other, to_at):
        return swap(share_out, share_in, share_send_sem, share_recv_sem, other, other, to_at)

    for other in leave_order:
        query_copy(other, rank, rank).start()

    def block(owner, i):
        kv = (owner * heads_here + i * per) // group
        at = pl.ds(pl.multiple_of(kv * LANES, LANES), LANES)
        query = jnp.concatenate(
            [
                queries[owner, :, (i * per + h) * LANES : (i * per + h + 1) * LANES]
                for h in range(per)
            ],
            axis=0,
        )
        key = keys[:, :, at].reshape(wide, LANES)
        value = values[:, :, at].reshape(wide, LANES)
        score = lax.dot_general(
            query, key, (((1,), (1,)), ((), ())), preferred_element_type=jnp.float32
        )
        table = scale_rows[...]
        key_scale = jnp.sum(jnp.where(lane == kv, table, 0.0), axis=1, keepdims=True)
        value_at = kv + gain_ref.shape[1] // 2
        value_scale = jnp.sum(jnp.where(lane == value_at, table, 0.0), axis=1, keepdims=True)
        valid = bias[...] == 0.0
        score = jnp.where(valid, score * key_scale, NEGATIVE)
        peak = jnp.max(score, axis=1, keepdims=True)
        weight = jnp.where(valid, jnp.exp(score - peak), 0.0)
        total = jnp.sum(weight, axis=1, keepdims=True)
        out = jnp.dot(weight.astype(jnp.bfloat16), value, preferred_element_type=jnp.float32)
        stat = jnp.where(lane == 0, peak, jnp.where(lane == 1, total, 0.0))
        return out * value_scale, stat

    for i in range(kv_here):
        at = slice(i * tall, (i + 1) * tall)
        part_own[at, :], stat_own[at, :] = block(rank, i)

    for other in arrive_order:
        query_copy(other, rank, other).wait_recv()
        for i in range(kv_here):
            at = slice(i * tall, (i + 1) * tall)
            out, stat = block(other, i)
            part_out[other, at, :] = out.astype(jnp.bfloat16)
            stat_out[other, :, at] = stat.T[:8]
        stat_copy(other, rank).start()
        part_copy(other, rank).start()

    top = stat_own[:, 0:1]
    total = stat_own[:, 1:2]
    summed = part_own[...]
    for other in arrive_order:
        stat_copy(other, other).wait_recv()
        part_copy(other, other).wait_recv()
        stat = stat_in[other].T
        peak = stat[:, 0:1]
        now = jnp.maximum(top, peak)
        left = jnp.exp(top - now)
        right = jnp.exp(peak - now)
        total = total * left + stat[:, 1:2] * right
        summed = summed * left + part_in[other].astype(jnp.float32) * right
        top = now
    merged = (summed / total).astype(jnp.bfloat16)
    for h in range(heads_here):
        attended[:, h * LANES : (h + 1) * LANES] = merged[h * rows : (h + 1) * rows]

    @pl.loop(0, chunks)
    def _(c):
        load_ow(c).wait()

    tile = min(share, 512)

    def terms(owner, j):
        at = pl.ds(pl.multiple_of(owner * share + j * tile, LANES), tile)
        return jnp.dot(attended[...], ow[:, at], preferred_element_type=jnp.float32)

    for other in leave_order:
        for j in range(share // tile):
            share_out[other, :, j * tile : (j + 1) * tile] = terms(other, j).astype(jnp.bfloat16)
        share_copy(other, rank).start()
    for j in range(share // tile):
        share_own[:, j * tile : (j + 1) * tile] = terms(rank, j)

    stored = []
    sources = []
    for j in range(moves):
        source = jnp.int32(0)
        for s in range(replicas):
            source = jnp.where(dest_ref[s, j] == here, s, source)
        sources.append(source)
    plan = []
    for r in range(held):
        source = here
        for j in range(moves):
            source = jnp.where(slots[j] == r, sources[j], source)
        plan.append(source)

    def place(which, old, new_hbm):
        for k in range(replicas - 1):
            take_codes(which, k).wait_recv()
        for r in range(held):
            placed[which, r] = jnp.where(plan[r] == here, old[r], recv_codes[which][plan[r]])
        out = pltpu.make_async_copy(placed.at[which], new_hbm, out_sem.at[which])
        out.start()
        stored.append(out)

    place(0, keys, new_keys_hbm)

    total = share_own[...]
    for other in arrive_order:
        share_copy(other, other).wait_recv()
        total = total + share_in[other].astype(jnp.float32)
    gate = jnp.tanh(jnp.full((1, LANES), gate_ref[0], jnp.float32))[:, 0:1]
    at = pl.ds(pl.multiple_of(rank * share, LANES), share)
    mixed_ref[...] = (hidden[:, at].astype(jnp.float32) + gate * total).astype(jnp.bfloat16)

    place(1, values, new_values_hbm)
    for k in range(replicas - 1):
        move_scale(k, far[k]).wait_recv()
    for r in range(held):
        new_scale_ref[r] = jnp.where(
            plan[r] == here, scale_ref[r], recv_scale[plan[r]][0:1]
        )

    for k in range(replicas - 1):
        move_codes(0, k).wait_send()
        move_codes(1, k).wait_send()
        move_scale(k, here).wait_send()
    for other in leave_order:
        query_copy(other, rank, rank).wait_send()
        stat_copy(other, rank).wait_send()
        part_copy(other, rank).wait_send()
        share_copy(other, rank).wait_send()
    for out in stored:
        out.wait()


def local(
    replicas,
    shards,
    hidden,
    q_weight,
    q_gain,
    o_weight,
    attn_gate,
    key_codes,
    value_codes,
    key_scales,
    value_scales,
    lengths,
    dest_replica,
    move_slot,
):
    held, span, kv_width = key_codes.shape
    kv_heads = key_scales.shape[2]
    rows, width = hidden.shape
    out_width = q_weight.shape[1]
    heads_here = out_width // LANES
    group = heads_here * shards // kv_heads
    tall = heads_here * rows
    short = min(heads_here, group) * rows
    chunks = 16
    half = LANES // 2
    share = width // shards
    scales = jnp.concatenate(
        [
            jnp.pad(s.astype(jnp.float32), ((0, 0), (0, 0), (0, half - kv_heads)))
            for s in (key_scales, value_scales)
        ],
        axis=2,
    )
    vmem = pl.BlockSpec(memory_space=pltpu.VMEM)
    smem = pl.BlockSpec(memory_space=pltpu.SMEM)
    anywhere = pl.BlockSpec(memory_space=pl.ANY)
    bf16, f32 = jnp.bfloat16, jnp.float32
    dma = pltpu.SemaphoreType.DMA
    mixed, new_keys, new_values, new_scales = pl.pallas_call(
        functools.partial(kernel, replicas, shards, heads_here, group, chunks),
        out_shape=(
            jax.ShapeDtypeStruct((rows, share), bf16),
            jax.ShapeDtypeStruct(key_codes.shape, bf16),
            jax.ShapeDtypeStruct(key_codes.shape, bf16),
            jax.ShapeDtypeStruct(scales.shape, f32),
        ),
        in_specs=[smem] * 4 + [vmem] * 2 + [anywhere] * 5,
        out_specs=(vmem, anywhere, anywhere, vmem),
        scratch_shapes=[
            pltpu.VMEM(hidden.shape, bf16),
            pltpu.VMEM(q_weight.shape, bf16),
            pltpu.VMEM(o_weight.shape, bf16),
            pltpu.VMEM(key_codes.shape, bf16),
            pltpu.VMEM(key_codes.shape, bf16),
            pltpu.VMEM((2, replicas, span, kv_width), bf16),
            pltpu.VMEM((replicas, span, kv_width), bf16),
            pltpu.VMEM((replicas, span, kv_width), bf16),
            pltpu.VMEM((replicas, 8, LANES), f32),
            pltpu.VMEM((replicas, 8, LANES), f32),
            pltpu.VMEM((2,) + key_codes.shape, bf16),
            pltpu.VMEM((rows, out_width), f32),
            pltpu.VMEM((shards, rows, out_width), bf16),
            pltpu.VMEM((tall, LANES), f32),
            pltpu.VMEM((shards, tall, LANES), bf16),
            pltpu.VMEM((shards, tall, LANES), bf16),
            pltpu.VMEM((tall, LANES), f32),
            pltpu.VMEM((shards, 8, tall), f32),
            pltpu.VMEM((shards, 8, tall), f32),
            pltpu.VMEM((rows, out_width), bf16),
            pltpu.VMEM((rows, share), f32),
            pltpu.VMEM((shards, rows, share), bf16),
            pltpu.VMEM((shards, rows, share), bf16),
            pltpu.VMEM((short, LANES), f32),
            pltpu.VMEM((short, held * span), f32),
            dma((3,)),
            dma((chunks,)),
            dma((chunks,)),
            dma((2, replicas)),
            dma((2, replicas)),
            dma((replicas,)),
            dma((replicas,)),
            dma((shards,)),
            dma((shards,)),
            dma((shards,)),
            dma((shards,)),
            dma((shards,)),
            dma((shards,)),
            dma((shards,)),
            dma((shards,)),
            dma((2,)),
        ],
        compiler_params=pltpu.CompilerParams(
            collective_id=0, has_side_effects=True, vmem_limit_bytes=60 * 2**20
        ),
    )(
        dest_replica,
        move_slot,
        lengths,
        attn_gate,
        q_gain.reshape(1, LANES),
        scales,
        hidden,
        q_weight,
        o_weight,
        key_codes,
        value_codes,
    )
    new_key_scales = new_scales[:, :, :kv_heads].astype(bf16)
    new_value_scales = new_scales[:, :, half : half + kv_heads].astype(bf16)
    return (mixed, new_keys, new_values, new_key_scales, new_value_scales)


def solution(mesh):
    return jax.shard_map(
        functools.partial(local, mesh.shape["replica"], mesh.shape["tensor"]),
        mesh=mesh,
        in_specs=(
            P("replica", None),
            P(None, "tensor"),
            P(),
            P("tensor", None),
            P(),
            P("replica", "tensor", None),
            P("replica", "tensor", None),
            P("replica", "tensor", None),
            P("replica", "tensor", None),
            P("replica"),
            P(),
            P("replica", None),
        ),
        out_specs=(
            P("replica", "tensor"),
            P("replica", "tensor", None),
            P("replica", "tensor", None),
            P("replica", "tensor", None),
            P("replica", "tensor", None),
        ),
        check_vma=False,
    )
```

```python
import functools

import jax
import jax.numpy as jnp
from jax import lax
from jax.experimental import pallas as pl
from jax.experimental.pallas import tpu as pltpu
from jax.sharding import PartitionSpec as P

NEGATIVE = -1e30
EPSILON = 1e-06
LANES = 128
MESH = pl.DeviceIdType.MESH


def kernel(
    replicas,
    shards,
    heads_here,
    group,
    chunks,
    dest_ref,
    slot_ref,
    len_ref,
    gate_ref,
    gain_ref,
    key_scale_ref,
    value_scale_ref,
    hidden_hbm,
    qw_hbm,
    ow_hbm,
    keys_hbm,
    values_hbm,
    mixed_ref,
    new_keys,
    new_values,
    new_key_scale_ref,
    new_value_scale_ref,
    hidden,
    qw,
    ow,
    keys,
    values,
    send_codes,
    recv_keys,
    recv_values,
    send_scale,
    recv_scale,
    scale_ref,
    scale_out,
    acc,
    queries,
    part_own,
    part_out,
    part_in,
    stat_own,
    stat_out,
    stat_in,
    attended,
    share_own,
    share_out,
    share_in,
    key_rows,
    value_rows,
    bias,
    load_sem,
    qw_sem,
    ow_sem,
    code_send_sem,
    code_recv_sem,
    scale_send_sem,
    scale_recv_sem,
    query_send_sem,
    query_recv_sem,
    part_send_sem,
    part_recv_sem,
    stat_send_sem,
    stat_recv_sem,
    share_send_sem,
    share_recv_sem,
):
    here = lax.axis_index("replica")
    rank = lax.axis_index("tensor")
    held, span, _ = keys.shape
    moves = slot_ref.shape[1]
    rows, width = hidden.shape
    drafts = rows // held
    per = min(heads_here, group)
    kv_here = heads_here // per
    tall = per * rows
    deep = qw_hbm.shape[0] // chunks
    high = ow_hbm.shape[0] // chunks
    share = width // shards

    loads = [
        pltpu.make_async_copy(keys_hbm, keys, load_sem.at[0]),
        pltpu.make_async_copy(values_hbm, values, load_sem.at[1]),
        pltpu.make_async_copy(hidden_hbm, hidden, load_sem.at[2]),
    ]
    for load in loads:
        load.start()

    def load_qw(c):
        at = pl.ds(pl.multiple_of(c * deep, deep), deep)
        return pltpu.make_async_copy(qw_hbm.at[at], qw.at[at], qw_sem.at[c])

    def load_ow(c):
        at = pl.ds(pl.multiple_of(c * high, high), high)
        return pltpu.make_async_copy(ow_hbm.at[at], ow.at[at], ow_sem.at[c])

    for c in range(chunks):
        load_qw(c).start()

    far = [lax.rem(here + k, replicas) for k in range(1, replicas)]
    partner = rank + 1 - 2 * lax.rem(rank, 2)
    near = []
    for j in range(1, shards // 2):
        pair = lax.rem(rank // 2 + j, shards // 2) * 2
        near += [pair + lax.rem(rank + c, 2) for c in range(2)]
    arrive_order = [partner] + near
    leave_order = near + [partner]

    barrier = pltpu.get_barrier_semaphore()
    for other in far:
        pl.semaphore_signal(barrier, inc=1, device_id=(other, rank), device_id_type=MESH)
    for other in leave_order:
        pl.semaphore_signal(barrier, inc=1, device_id=(here, other), device_id_type=MESH)

    slots = [slot_ref[0, j] for j in range(moves)]

    def leaving(target):
        found = jnp.int32(0)
        for j in range(moves):
            found = jnp.where(dest_ref[here, j] == target, slots[j], found)
        return found

    kv_heads = key_scale_ref.shape[1]
    scale_ref[...] = jnp.zeros_like(scale_ref)
    for which, ref in enumerate((key_scale_ref, value_scale_ref)):
        whole = ref[...].astype(jnp.float32)
        for r in range(held):
            scale_ref[r, which : which + 1, 0:kv_heads] = whole[r : r + 1]

    loads[0].wait()
    loads[1].wait()
    for other in far:
        slot = leaving(other)
        send_codes[0, other] = keys[slot]
        send_codes[1, other] = values[slot]
        send_scale[other] = scale_ref[slot]
    recv_codes = (recv_keys, recv_values)
    recv_keys[here] = keys[0]
    recv_values[here] = values[0]
    recv_scale[here] = scale_ref[0]

    pl.semaphore_wait(barrier, replicas - 1 + shards - 1)

    def move_codes(which, k):
        other = far[k]
        return pltpu.make_async_remote_copy(
            src_ref=send_codes.at[which, other],
            dst_ref=recv_codes[which].at[here],
            send_sem=code_send_sem.at[which, other],
            recv_sem=code_recv_sem.at[which, here],
            device_id=(other, rank),
            device_id_type=MESH,
        )

    def take_codes(which, k):
        other = far[k]
        return pltpu.make_async_remote_copy(
            src_ref=send_codes.at[which, other],
            dst_ref=recv_codes[which].at[other],
            send_sem=code_send_sem.at[which, other],
            recv_sem=code_recv_sem.at[which, other],
            device_id=(other, rank),
            device_id_type=MESH,
        )

    def move_scale(k, at):
        other = far[k]
        return pltpu.make_async_remote_copy(
            src_ref=send_scale.at[other],
            dst_ref=recv_scale.at[at],
            send_sem=scale_send_sem.at[other],
            recv_sem=scale_recv_sem.at[at],
            device_id=(other, rank),
            device_id_type=MESH,
        )

    for which in range(2):
        for k in range(replicas - 1):
            move_codes(which, k).start()
    for k in range(replicas - 1):
        move_scale(k, here).start()

    lane = lax.broadcasted_iota(jnp.int32, (tall, LANES), 1)
    row_request = lax.rem(lax.broadcasted_iota(jnp.int32, (tall, LANES), 0), rows) // drafts
    for which, scale_rows in enumerate((key_rows, value_rows)):
        table = jnp.zeros((tall, LANES), jnp.float32)
        for r in range(held):
            table = jnp.where(row_request == r, scale_ref[r, which : which + 1], table)
        scale_rows[...] = table
    wide = held * span
    column = lax.broadcasted_iota(jnp.int32, (tall, wide), 1)
    column_request = column // span
    row_of = lax.rem(lax.broadcasted_iota(jnp.int32, (tall, wide), 0), rows) // drafts
    limit = jnp.zeros((tall, wide), jnp.int32)
    for r in range(held):
        limit = jnp.where(column_request == r, len_ref[r], limit)
    position = rank * span + lax.rem(column, span)
    bias[...] = jnp.where((position < limit) & (row_of == column_request), 0.0, NEGATIVE)

    loads[2].wait()
    acc[...] = jnp.zeros_like(acc)

    @pl.loop(0, chunks)
    def _(c):
        load_qw(c).wait()
        load_ow(c).start()
        at = pl.ds(pl.multiple_of(c * deep, deep), deep)
        acc[...] += jnp.dot(hidden[:, at], qw[at, :], preferred_element_type=jnp.float32)

    for h in range(heads_here):
        at = slice(h * LANES, (h + 1) * LANES)
        head = acc[:, at]
        head = head * lax.rsqrt(jnp.mean(head * head, axis=-1, keepdims=True) + EPSILON)
        queries[rank, :, at] = (head * gain_ref[...] * LANES ** (-0.5)).astype(jnp.bfloat16)

    def swap(source, target, send_sem, recv_sem, other, from_at, to_at):
        return pltpu.make_async_remote_copy(
            src_ref=source.at[from_at],
            dst_ref=target.at[to_at],
            send_sem=send_sem.at[other],
            recv_sem=recv_sem.at[to_at],
            device_id=(here, other),
            device_id_type=MESH,
        )

    def query_copy(other, from_at, to_at):
        return swap(queries, queries, query_send_sem, query_recv_sem, other, from_at, to_at)

    def part_copy(other, to_at):
        return swap(part_out, part_in, part_send_sem, part_recv_sem, other, other, to_at)

    def stat_copy(other, to_at):
        return swap(stat_out, stat_in, stat_send_sem, stat_recv_sem, other, other, to_at)

    def share_copy(other, to_at):
        return swap(share_out, share_in, share_send_sem, share_recv_sem, other, other, to_at)

    for other in leave_order:
        query_copy(other, rank, rank).start()

    def block(owner, i):
        kv = (owner * heads_here + i * per) // group
        at = pl.ds(pl.multiple_of(kv * LANES, LANES), LANES)
        query = jnp.concatenate(
            [
                queries[owner, :, (i * per + h) * LANES : (i * per + h + 1) * LANES]
                for h in range(per)
            ],
            axis=0,
        )
        key = keys[:, :, at].reshape(wide, LANES)
        value = values[:, :, at].reshape(wide, LANES)
        score = lax.dot_general(
            query, key, (((1,), (1,)), ((), ())), preferred_element_type=jnp.float32
        )
        chosen = lane == kv
        key_scale = jnp.sum(jnp.where(chosen, key_rows[...], 0.0), axis=1, keepdims=True)
        value_scale = jnp.sum(jnp.where(chosen, value_rows[...], 0.0), axis=1, keepdims=True)
        valid = bias[...] == 0.0
        score = jnp.where(valid, score * key_scale, NEGATIVE)
        peak = jnp.max(score, axis=1, keepdims=True)
        weight = jnp.where(valid, jnp.exp(score - peak), 0.0)
        total = jnp.sum(weight, axis=1, keepdims=True)
        out = jnp.dot(weight.astype(jnp.bfloat16), value, preferred_element_type=jnp.float32)
        stat = jnp.where(lane == 0, peak, jnp.where(lane == 1, total, 0.0))
        return out * value_scale, stat

    for i in range(kv_here):
        at = slice(i * tall, (i + 1) * tall)
        part_own[at, :], stat_own[at, :] = block(rank, i)

    for other in arrive_order:
        query_copy(other, rank, other).wait_recv()
        for i in range(kv_here):
            at = slice(i * tall, (i + 1) * tall)
            out, stat = block(other, i)
            part_out[other, at, :] = out.astype(jnp.bfloat16)
            stat_out[other, :, at] = stat.T[:8]
        stat_copy(other, rank).start()
        part_copy(other, rank).start()

    top = stat_own[:, 0:1]
    total = stat_own[:, 1:2]
    summed = part_own[...]
    for other in arrive_order:
        stat_copy(other, other).wait_recv()
        part_copy(other, other).wait_recv()
        stat = stat_in[other].T
        peak = stat[:, 0:1]
        now = jnp.maximum(top, peak)
        left = jnp.exp(top - now)
        right = jnp.exp(peak - now)
        total = total * left + stat[:, 1:2] * right
        summed = summed * left + part_in[other].astype(jnp.float32) * right
        top = now
    merged = (summed / total).astype(jnp.bfloat16)
    for h in range(heads_here):
        attended[:, h * LANES : (h + 1) * LANES] = merged[h * rows : (h + 1) * rows]

    @pl.loop(0, chunks)
    def _(c):
        load_ow(c).wait()

    tile = min(share, 512)

    def terms(owner, j):
        at = pl.ds(pl.multiple_of(owner * share + j * tile, LANES), tile)
        return jnp.dot(attended[...], ow[:, at], preferred_element_type=jnp.float32)

    for other in leave_order:
        for j in range(share // tile):
            share_out[other, :, j * tile : (j + 1) * tile] = terms(other, j).astype(jnp.bfloat16)
        share_copy(other, rank).start()
    for j in range(share // tile):
        share_own[:, j * tile : (j + 1) * tile] = terms(rank, j)

    sources = []
    for j in range(moves):
        source = jnp.int32(0)
        for s in range(replicas):
            source = jnp.where(dest_ref[s, j] == here, s, source)
        sources.append(source)
    plan = []
    for r in range(held):
        source = here
        for j in range(moves):
            source = jnp.where(slots[j] == r, sources[j], source)
        plan.append(source)

    def place(which, old, new):
        for k in range(replicas - 1):
            take_codes(which, k).wait_recv()
        for r in range(held):
            new[r] = jnp.where(plan[r] == here, old[r], recv_codes[which][plan[r]])

    place(0, keys, new_keys)

    total = share_own[...]
    for other in arrive_order:
        share_copy(other, other).wait_recv()
        total = total + share_in[other].astype(jnp.float32)
    gate = jnp.tanh(jnp.full((1, LANES), gate_ref[0], jnp.float32))[:, 0:1]
    at = pl.ds(pl.multiple_of(rank * share, LANES), share)
    mixed_ref[...] = (hidden[:, at].astype(jnp.float32) + gate * total).astype(jnp.bfloat16)

    place(1, values, new_values)
    for k in range(replicas - 1):
        move_scale(k, far[k]).wait_recv()
    for r in range(held):
        row = jnp.where(plan[r] == here, scale_ref[r], recv_scale[plan[r]])
        scale_out[0, r : r + 1] = row[0:1]
        scale_out[1, r : r + 1] = row[1:2]
    new_key_scale_ref[...] = scale_out[0][:, :kv_heads].astype(jnp.bfloat16)
    new_value_scale_ref[...] = scale_out[1][:, :kv_heads].astype(jnp.bfloat16)

    for k in range(replicas - 1):
        move_codes(0, k).wait_send()
        move_codes(1, k).wait_send()
        move_scale(k, here).wait_send()
    for other in leave_order:
        query_copy(other, rank, rank).wait_send()
        stat_copy(other, rank).wait_send()
        part_copy(other, rank).wait_send()
        share_copy(other, rank).wait_send()


def store_out(*refs):
    count = (len(refs) - 1) // 2
    sem = refs[-1]
    copies = [
        pltpu.make_async_copy(refs[i], refs[count + i], sem.at[i]) for i in range(count)
    ]
    for copy in copies:
        copy.start()
    for copy in copies:
        copy.wait()


def local(
    replicas,
    shards,
    hidden,
    q_weight,
    q_gain,
    o_weight,
    attn_gate,
    key_codes,
    value_codes,
    key_scales,
    value_scales,
    lengths,
    dest_replica,
    move_slot,
):
    held, span, kv_width = key_codes.shape
    kv_heads = key_scales.shape[2]
    rows, width = hidden.shape
    out_width = q_weight.shape[1]
    heads_here = out_width // LANES
    group = heads_here * shards // kv_heads
    tall = heads_here * rows
    short = min(heads_here, group) * rows
    chunks = 16
    share = width // shards
    vmem = pl.BlockSpec(memory_space=pltpu.VMEM)
    smem = pl.BlockSpec(memory_space=pltpu.SMEM)
    anywhere = pl.BlockSpec(memory_space=pl.ANY)
    bf16, f32 = jnp.bfloat16, jnp.float32
    dma = pltpu.SemaphoreType.DMA
    results = (
        ((rows, share), bf16),
        (key_codes.shape, bf16),
        (key_codes.shape, bf16),
        ((held, kv_heads), bf16),
        ((held, kv_heads), bf16),
    )
    staged = pl.pallas_call(
        functools.partial(kernel, replicas, shards, heads_here, group, chunks),
        out_shape=tuple(pltpu.VMEM(shape, kind) for shape, kind in results),
        in_specs=[smem] * 4 + [vmem] * 3 + [anywhere] * 5,
        out_specs=(vmem,) * 5,
        scratch_shapes=[
            pltpu.VMEM(hidden.shape, bf16),
            pltpu.VMEM(q_weight.shape, bf16),
            pltpu.VMEM(o_weight.shape, bf16),
            pltpu.VMEM(key_codes.shape, bf16),
            pltpu.VMEM(key_codes.shape, bf16),
            pltpu.VMEM((2, replicas, span, kv_width), bf16),
            pltpu.VMEM((replicas, span, kv_width), bf16),
            pltpu.VMEM((replicas, span, kv_width), bf16),
            pltpu.VMEM((replicas, 8, LANES), f32),
            pltpu.VMEM((replicas, 8, LANES), f32),
            pltpu.VMEM((held, 8, LANES), f32),
            pltpu.VMEM((2, held, LANES), f32),
            pltpu.VMEM((rows, out_width), f32),
            pltpu.VMEM((shards, rows, out_width), bf16),
            pltpu.VMEM((tall, LANES), f32),
            pltpu.VMEM((shards, tall, LANES), bf16),
            pltpu.VMEM((shards, tall, LANES), bf16),
            pltpu.VMEM((tall, LANES), f32),
            pltpu.VMEM((shards, 8, tall), f32),
            pltpu.VMEM((shards, 8, tall), f32),
            pltpu.VMEM((rows, out_width), bf16),
            pltpu.VMEM((rows, share), f32),
            pltpu.VMEM((shards, rows, share), bf16),
            pltpu.VMEM((shards, rows, share), bf16),
            pltpu.VMEM((short, LANES), f32),
            pltpu.VMEM((short, LANES), f32),
            pltpu.VMEM((short, held * span), f32),
            dma((3,)),
            dma((chunks,)),
            dma((chunks,)),
            dma((2, replicas)),
            dma((2, replicas)),
            dma((replicas,)),
            dma((replicas,)),
            dma((shards,)),
            dma((shards,)),
            dma((shards,)),
            dma((shards,)),
            dma((shards,)),
            dma((shards,)),
            dma((shards,)),
            dma((shards,)),
        ],
        compiler_params=pltpu.CompilerParams(
            collective_id=0, has_side_effects=True, vmem_limit_bytes=60 * 2**20
        ),
    )(
        dest_replica,
        move_slot,
        lengths,
        attn_gate,
        q_gain.reshape(1, LANES),
        key_scales.reshape(held, kv_heads),
        value_scales.reshape(held, kv_heads),
        hidden,
        q_weight,
        o_weight,
        key_codes,
        value_codes,
    )
    mixed, new_keys, new_values, new_key_scales, new_value_scales = pl.pallas_call(
        store_out,
        out_shape=tuple(jax.ShapeDtypeStruct(shape, kind) for shape, kind in results),
        in_specs=[vmem] * len(results),
        out_specs=(anywhere,) * len(results),
        scratch_shapes=[dma((len(results),))],
    )(*[pltpu.with_memory_space_constraint(x, pltpu.VMEM) for x in staged])
    return (
        mixed,
        new_keys,
        new_values,
        new_key_scales.reshape(key_scales.shape),
        new_value_scales.reshape(value_scales.shape),
    )


def solution(mesh):
    return jax.shard_map(
        functools.partial(local, mesh.shape["replica"], mesh.shape["tensor"]),
        mesh=mesh,
        in_specs=(
            P("replica", None),
            P(None, "tensor"),
            P(),
            P("tensor", None),
            P(),
            P("replica", "tensor", None),
            P("replica", "tensor", None),
            P("replica", "tensor", None),
            P("replica", "tensor", None),
            P("replica"),
            P(),
            P("replica", None),
        ),
        out_specs=(
            P("replica", "tensor"),
            P("replica", "tensor", None),
            P("replica", "tensor", None),
            P("replica", "tensor", None),
            P("replica", "tensor", None),
        ),
        check_vma=False,
    )
```

```python
import functools

import jax
import jax.numpy as jnp
from jax import lax
from jax.experimental import pallas as pl
from jax.experimental.pallas import tpu as pltpu
from jax.sharding import PartitionSpec as P

NEGATIVE = -1e30
EPSILON = 1e-06
LANES = 128
MESH = pl.DeviceIdType.MESH


def kernel(
    replicas,
    shards,
    heads_here,
    group,
    chunks,
    dest_ref,
    slot_ref,
    len_ref,
    gate_ref,
    gain_ref,
    key_scale_ref,
    value_scale_ref,
    hidden_hbm,
    qw_hbm,
    ow_hbm,
    keys_hbm,
    values_hbm,
    mixed_ref,
    new_keys,
    new_values,
    new_key_scale_ref,
    new_value_scale_ref,
    hidden,
    qw,
    ow,
    keys,
    values,
    send_codes,
    recv_keys,
    recv_values,
    send_scale,
    recv_scale,
    scale_ref,
    scale_out,
    acc,
    queries,
    part_own,
    part_out,
    part_in,
    stat_own,
    stat_out,
    stat_in,
    attended,
    share_own,
    share_out,
    share_in,
    key_rows,
    value_rows,
    bias,
    load_sem,
    qw_sem,
    ow_sem,
    code_send_sem,
    code_recv_sem,
    scale_send_sem,
    scale_recv_sem,
    query_send_sem,
    query_recv_sem,
    part_send_sem,
    part_recv_sem,
    stat_send_sem,
    stat_recv_sem,
    share_send_sem,
    share_recv_sem,
):
    here = lax.axis_index("replica")
    rank = lax.axis_index("tensor")
    held, span, _ = keys.shape
    moves = slot_ref.shape[1]
    rows, width = hidden.shape
    drafts = rows // held
    per = min(heads_here, group)
    kv_here = heads_here // per
    tall = per * rows
    deep = qw_hbm.shape[0] // chunks
    high = ow_hbm.shape[0] // chunks
    share = width // shards

    loads = [
        pltpu.make_async_copy(keys_hbm, keys, load_sem.at[0]),
        pltpu.make_async_copy(values_hbm, values, load_sem.at[1]),
        pltpu.make_async_copy(hidden_hbm, hidden, load_sem.at[2]),
    ]
    for load in loads[:2]:
        load.start()

    def load_qw(c):
        at = pl.ds(pl.multiple_of(c * deep, deep), deep)
        return pltpu.make_async_copy(qw_hbm.at[at], qw.at[at], qw_sem.at[c])

    def load_ow(c):
        at = pl.ds(pl.multiple_of(c * high, high), high)
        return pltpu.make_async_copy(ow_hbm.at[at], ow.at[at], ow_sem.at[c])

    far = [lax.rem(here + k, replicas) for k in range(1, replicas)]
    partner = rank + 1 - 2 * lax.rem(rank, 2)
    near = []
    for j in range(1, shards // 2):
        pair = lax.rem(rank // 2 + j, shards // 2) * 2
        near += [pair + lax.rem(rank + c, 2) for c in range(2)]
    arrive_order = [partner] + near
    leave_order = near + [partner]

    barrier = pltpu.get_barrier_semaphore()
    for other in far:
        pl.semaphore_signal(barrier, inc=1, device_id=(other, rank), device_id_type=MESH)
    for other in leave_order:
        pl.semaphore_signal(barrier, inc=1, device_id=(here, other), device_id_type=MESH)

    slots = [slot_ref[0, j] for j in range(moves)]

    def leaving(target):
        found = jnp.int32(0)
        for j in range(moves):
            found = jnp.where(dest_ref[here, j] == target, slots[j], found)
        return found

    kv_heads = key_scale_ref.shape[1]
    scale_ref[...] = jnp.zeros_like(scale_ref)
    for which, ref in enumerate((key_scale_ref, value_scale_ref)):
        whole = ref[...].astype(jnp.float32)
        for r in range(held):
            scale_ref[r, which : which + 1, 0:kv_heads] = whole[r : r + 1]

    loads[0].wait()
    loads[1].wait()
    loads[2].start()
    for c in range(chunks):
        load_qw(c).start()
    for other in far:
        slot = leaving(other)
        send_codes[0, other] = keys[slot]
        send_codes[1, other] = values[slot]
        send_scale[other] = scale_ref[slot]
    recv_codes = (recv_keys, recv_values)
    recv_keys[here] = keys[0]
    recv_values[here] = values[0]
    recv_scale[here] = scale_ref[0]

    pl.semaphore_wait(barrier, replicas - 1 + shards - 1)

    def move_codes(which, k):
        other = far[k]
        return pltpu.make_async_remote_copy(
            src_ref=send_codes.at[which, other],
            dst_ref=recv_codes[which].at[here],
            send_sem=code_send_sem.at[which, other],
            recv_sem=code_recv_sem.at[which, here],
            device_id=(other, rank),
            device_id_type=MESH,
        )

    def take_codes(which, k):
        other = far[k]
        return pltpu.make_async_remote_copy(
            src_ref=send_codes.at[which, other],
            dst_ref=recv_codes[which].at[other],
            send_sem=code_send_sem.at[which, other],
            recv_sem=code_recv_sem.at[which, other],
            device_id=(other, rank),
            device_id_type=MESH,
        )

    def move_scale(k, at):
        other = far[k]
        return pltpu.make_async_remote_copy(
            src_ref=send_scale.at[other],
            dst_ref=recv_scale.at[at],
            send_sem=scale_send_sem.at[other],
            recv_sem=scale_recv_sem.at[at],
            device_id=(other, rank),
            device_id_type=MESH,
        )

    for which in range(2):
        for k in range(replicas - 1):
            move_codes(which, k).start()
    for k in range(replicas - 1):
        move_scale(k, here).start()

    lane = lax.broadcasted_iota(jnp.int32, (tall, LANES), 1)
    row_request = lax.rem(lax.broadcasted_iota(jnp.int32, (tall, LANES), 0), rows) // drafts
    for which, scale_rows in enumerate((key_rows, value_rows)):
        table = jnp.zeros((tall, LANES), jnp.float32)
        for r in range(held):
            table = jnp.where(row_request == r, scale_ref[r, which : which + 1], table)
        scale_rows[...] = table
    wide = held * span
    column = lax.broadcasted_iota(jnp.int32, (tall, wide), 1)
    column_request = column // span
    row_of = lax.rem(lax.broadcasted_iota(jnp.int32, (tall, wide), 0), rows) // drafts
    limit = jnp.zeros((tall, wide), jnp.int32)
    for r in range(held):
        limit = jnp.where(column_request == r, len_ref[r], limit)
    position = rank * span + lax.rem(column, span)
    bias[...] = jnp.where((position < limit) & (row_of == column_request), 0.0, NEGATIVE)

    loads[2].wait()
    acc[...] = jnp.zeros_like(acc)

    @pl.loop(0, chunks)
    def _(c):
        load_qw(c).wait()
        at = pl.ds(pl.multiple_of(c * deep, deep), deep)
        acc[...] += jnp.dot(hidden[:, at], qw[at, :], preferred_element_type=jnp.float32)

    for c in range(chunks):
        load_ow(c).start()

    for h in range(heads_here):
        at = slice(h * LANES, (h + 1) * LANES)
        head = acc[:, at]
        head = head * lax.rsqrt(jnp.mean(head * head, axis=-1, keepdims=True) + EPSILON)
        queries[rank, :, at] = (head * gain_ref[...] * LANES ** (-0.5)).astype(jnp.bfloat16)

    def swap(source, target, send_sem, recv_sem, other, from_at, to_at):
        return pltpu.make_async_remote_copy(
            src_ref=source.at[from_at],
            dst_ref=target.at[to_at],
            send_sem=send_sem.at[other],
            recv_sem=recv_sem.at[to_at],
            device_id=(here, other),
            device_id_type=MESH,
        )

    def query_copy(other, from_at, to_at):
        return swap(queries, queries, query_send_sem, query_recv_sem, other, from_at, to_at)

    def part_copy(other, to_at):
        return swap(part_out, part_in, part_send_sem, part_recv_sem, other, other, to_at)

    def stat_copy(other, to_at):
        return swap(stat_out, stat_in, stat_send_sem, stat_recv_sem, other, other, to_at)

    def share_copy(other, to_at, j):
        return pltpu.make_async_remote_copy(
            src_ref=share_out.at[j, other],
            dst_ref=share_in.at[j, to_at],
            send_sem=share_send_sem.at[j, other],
            recv_sem=share_recv_sem.at[j, to_at],
            device_id=(here, other),
            device_id_type=MESH,
        )

    for other in leave_order:
        query_copy(other, rank, rank).start()

    def block(owner, i):
        kv = (owner * heads_here + i * per) // group
        at = pl.ds(pl.multiple_of(kv * LANES, LANES), LANES)
        query = jnp.concatenate(
            [
                queries[owner, :, (i * per + h) * LANES : (i * per + h + 1) * LANES]
                for h in range(per)
            ],
            axis=0,
        )
        key = keys[:, :, at].reshape(wide, LANES)
        value = values[:, :, at].reshape(wide, LANES)
        score = lax.dot_general(
            query, key, (((1,), (1,)), ((), ())), preferred_element_type=jnp.float32
        )
        chosen = lane == kv
        key_scale = jnp.sum(jnp.where(chosen, key_rows[...], 0.0), axis=1, keepdims=True)
        value_scale = jnp.sum(jnp.where(chosen, value_rows[...], 0.0), axis=1, keepdims=True)
        valid = bias[...] == 0.0
        score = jnp.where(valid, score * key_scale, NEGATIVE)
        peak = jnp.max(score, axis=1, keepdims=True)
        weight = jnp.where(valid, jnp.exp(score - peak), 0.0)
        total = jnp.sum(weight, axis=1, keepdims=True)
        out = jnp.dot(weight.astype(jnp.bfloat16), value, preferred_element_type=jnp.float32)
        stat = jnp.where(lane == 0, peak, jnp.where(lane == 1, total, 0.0))
        return out * value_scale, stat

    for i in range(kv_here):
        at = slice(i * tall, (i + 1) * tall)
        part_own[at, :], stat_own[at, :] = block(rank, i)

    for other in arrive_order:
        query_copy(other, rank, other).wait_recv()
        for i in range(kv_here):
            at = slice(i * tall, (i + 1) * tall)
            out, stat = block(other, i)
            part_out[other, at, :] = out.astype(jnp.bfloat16)
            stat_out[other, :, at] = stat.T[:8]
        stat_copy(other, rank).start()
        part_copy(other, rank).start()

    top = stat_own[:, 0:1]
    total = stat_own[:, 1:2]
    summed = part_own[...]
    for other in arrive_order:
        stat_copy(other, other).wait_recv()
        part_copy(other, other).wait_recv()
        stat = stat_in[other].T
        peak = stat[:, 0:1]
        now = jnp.maximum(top, peak)
        left = jnp.exp(top - now)
        right = jnp.exp(peak - now)
        total = total * left + stat[:, 1:2] * right
        summed = summed * left + part_in[other].astype(jnp.float32) * right
        top = now
    merged = (summed / total).astype(jnp.bfloat16)
    for h in range(heads_here):
        attended[:, h * LANES : (h + 1) * LANES] = merged[h * rows : (h + 1) * rows]

    @pl.loop(0, chunks)
    def _(c):
        load_ow(c).wait()

    tile = min(share, 512)

    def terms(owner, j):
        at = pl.ds(pl.multiple_of(owner * share + j * tile, LANES), tile)
        return jnp.dot(attended[...], ow[:, at], preferred_element_type=jnp.float32)

    for other in leave_order:
        for j in range(share // tile):
            share_out[j, other] = terms(other, j).astype(jnp.bfloat16)
            share_copy(other, rank, j).start()
    for j in range(share // tile):
        share_own[:, j * tile : (j + 1) * tile] = terms(rank, j)

    sources = []
    for j in range(moves):
        source = jnp.int32(0)
        for s in range(replicas):
            source = jnp.where(dest_ref[s, j] == here, s, source)
        sources.append(source)
    plan = []
    for r in range(held):
        source = here
        for j in range(moves):
            source = jnp.where(slots[j] == r, sources[j], source)
        plan.append(source)

    def place(which, old, new):
        for k in range(replicas - 1):
            take_codes(which, k).wait_recv()
        for r in range(held):
            new[r] = jnp.where(plan[r] == here, old[r], recv_codes[which][plan[r]])

    place(0, keys, new_keys)

    total = share_own[...]
    for other in arrive_order:
        for j in range(share // tile):
            share_copy(other, other, j).wait_recv()
        arrived = [share_in[j, other].astype(jnp.float32) for j in range(share // tile)]
        total = total + jnp.concatenate(arrived, axis=1)
    gate = jnp.tanh(jnp.full((1, LANES), gate_ref[0], jnp.float32))[:, 0:1]
    at = pl.ds(pl.multiple_of(rank * share, LANES), share)
    mixed_ref[...] = (hidden[:, at].astype(jnp.float32) + gate * total).astype(jnp.bfloat16)

    place(1, values, new_values)
    for k in range(replicas - 1):
        move_scale(k, far[k]).wait_recv()
    for r in range(held):
        row = jnp.where(plan[r] == here, scale_ref[r], recv_scale[plan[r]])
        scale_out[0, r : r + 1] = row[0:1]
        scale_out[1, r : r + 1] = row[1:2]
    new_key_scale_ref[...] = scale_out[0][:, :kv_heads].astype(jnp.bfloat16)
    new_value_scale_ref[...] = scale_out[1][:, :kv_heads].astype(jnp.bfloat16)

    for k in range(replicas - 1):
        move_codes(0, k).wait_send()
        move_codes(1, k).wait_send()
        move_scale(k, here).wait_send()
    for other in leave_order:
        query_copy(other, rank, rank).wait_send()
        stat_copy(other, rank).wait_send()
        part_copy(other, rank).wait_send()
        for j in range(share // tile):
            share_copy(other, rank, j).wait_send()


def store_out(*refs):
    count = (len(refs) - 1) // 2
    sem = refs[-1]
    copies = [
        pltpu.make_async_copy(refs[i], refs[count + i], sem.at[i]) for i in range(count)
    ]
    for copy in copies:
        copy.start()
    for copy in copies:
        copy.wait()


def local(
    replicas,
    shards,
    hidden,
    q_weight,
    q_gain,
    o_weight,
    attn_gate,
    key_codes,
    value_codes,
    key_scales,
    value_scales,
    lengths,
    dest_replica,
    move_slot,
):
    held, span, kv_width = key_codes.shape
    kv_heads = key_scales.shape[2]
    rows, width = hidden.shape
    out_width = q_weight.shape[1]
    heads_here = out_width // LANES
    group = heads_here * shards // kv_heads
    tall = heads_here * rows
    short = min(heads_here, group) * rows
    chunks = 16
    share = width // shards
    tile = min(share, 512)
    vmem = pl.BlockSpec(memory_space=pltpu.VMEM)
    smem = pl.BlockSpec(memory_space=pltpu.SMEM)
    anywhere = pl.BlockSpec(memory_space=pl.ANY)
    bf16, f32 = jnp.bfloat16, jnp.float32
    dma = pltpu.SemaphoreType.DMA
    results = (
        ((rows, share), bf16),
        (key_codes.shape, bf16),
        (key_codes.shape, bf16),
        ((held, kv_heads), bf16),
        ((held, kv_heads), bf16),
    )
    staged = pl.pallas_call(
        functools.partial(kernel, replicas, shards, heads_here, group, chunks),
        out_shape=tuple(pltpu.VMEM(shape, kind) for shape, kind in results),
        in_specs=[smem] * 4 + [vmem] * 3 + [anywhere] * 5,
        out_specs=(vmem,) * 5,
        scratch_shapes=[
            pltpu.VMEM(hidden.shape, bf16),
            pltpu.VMEM(q_weight.shape, bf16),
            pltpu.VMEM(o_weight.shape, bf16),
            pltpu.VMEM(key_codes.shape, bf16),
            pltpu.VMEM(key_codes.shape, bf16),
            pltpu.VMEM((2, replicas, span, kv_width), bf16),
            pltpu.VMEM((replicas, span, kv_width), bf16),
            pltpu.VMEM((replicas, span, kv_width), bf16),
            pltpu.VMEM((replicas, 8, LANES), f32),
            pltpu.VMEM((replicas, 8, LANES), f32),
            pltpu.VMEM((held, 8, LANES), f32),
            pltpu.VMEM((2, held, LANES), f32),
            pltpu.VMEM((rows, out_width), f32),
            pltpu.VMEM((shards, rows, out_width), bf16),
            pltpu.VMEM((tall, LANES), f32),
            pltpu.VMEM((shards, tall, LANES), bf16),
            pltpu.VMEM((shards, tall, LANES), bf16),
            pltpu.VMEM((tall, LANES), f32),
            pltpu.VMEM((shards, 8, tall), f32),
            pltpu.VMEM((shards, 8, tall), f32),
            pltpu.VMEM((rows, out_width), bf16),
            pltpu.VMEM((rows, share), f32),
            pltpu.VMEM((share // tile, shards, rows, tile), bf16),
            pltpu.VMEM((share // tile, shards, rows, tile), bf16),
            pltpu.VMEM((short, LANES), f32),
            pltpu.VMEM((short, LANES), f32),
            pltpu.VMEM((short, held * span), f32),
            dma((3,)),
            dma((chunks,)),
            dma((chunks,)),
            dma((2, replicas)),
            dma((2, replicas)),
            dma((replicas,)),
            dma((replicas,)),
            dma((shards,)),
            dma((shards,)),
            dma((shards,)),
            dma((shards,)),
            dma((shards,)),
            dma((shards,)),
            dma((share // tile, shards)),
            dma((share // tile, shards)),
        ],
        compiler_params=pltpu.CompilerParams(
            collective_id=0, has_side_effects=True, vmem_limit_bytes=60 * 2**20
        ),
    )(
        dest_replica,
        move_slot,
        lengths,
        attn_gate,
        q_gain.reshape(1, LANES),
        key_scales.reshape(held, kv_heads),
        value_scales.reshape(held, kv_heads),
        hidden,
        q_weight,
        o_weight,
        key_codes,
        value_codes,
    )
    mixed, new_keys, new_values, new_key_scales, new_value_scales = pl.pallas_call(
        store_out,
        out_shape=tuple(jax.ShapeDtypeStruct(shape, kind) for shape, kind in results),
        in_specs=[vmem] * len(results),
        out_specs=(anywhere,) * len(results),
        scratch_shapes=[dma((len(results),))],
    )(*[pltpu.with_memory_space_constraint(x, pltpu.VMEM) for x in staged])
    return (
        mixed,
        new_keys,
        new_values,
        new_key_scales.reshape(key_scales.shape),
        new_value_scales.reshape(value_scales.shape),
    )


def solution(mesh):
    return jax.shard_map(
        functools.partial(local, mesh.shape["replica"], mesh.shape["tensor"]),
        mesh=mesh,
        in_specs=(
            P("replica", None),
            P(None, "tensor"),
            P(),
            P("tensor", None),
            P(),
            P("replica", "tensor", None),
            P("replica", "tensor", None),
            P("replica", "tensor", None),
            P("replica", "tensor", None),
            P("replica"),
            P(),
            P("replica", None),
        ),
        out_specs=(
            P("replica", "tensor"),
            P("replica", "tensor", None),
            P("replica", "tensor", None),
            P("replica", "tensor", None),
            P("replica", "tensor", None),
        ),
        check_vma=False,
    )
```
